32 devices in a mesh: dp: 8 (over y, x, core), mp: 4 (over z).
Axes of the slice: x: 2, y: 2, z: 4, core: 2. Of those that a mesh axis runs over, the one named last changes fastest.
Arguments:
- tokens: bfloat16 [2, 1024, 4096], P(None, 'dp', 'mp'), may hold values from -6 to 6
- targets: bfloat16 [2, 1024, 4096], P(None, 'dp', 'mp'), may hold values from -6 to 6
- weight: bfloat16 [4096, 4096], P('mp'), may hold values from -0.09375 to 0.09375
- basis: bfloat16 [4096, 512], replicated, may hold values from -0.09375 to 0.09375
- moment1: float32 [4, 1024, 512], P('mp', 'dp'), may hold values from -0.06 to 0.06
- moment2: float32 [4, 1024, 512], P('mp', 'dp'), may hold values from 1e-05 to 0.001
Outputs:
- new_weight: bfloat16 [4096, 4096], P('mp')
- new_moment1: float32 [4, 1024, 512], P('mp', 'dp')
- new_moment2: float32 [4, 1024, 512], P('mp', 'dp')
The draws below stay inside these ranges and needn't reach their ends.
All inputs are finite; a program needn't handle non-finite values.
Results may differ from the reference program's by a relative error of at most 0.009.
Values may be sent and summed in bfloat16 or wider, within the bound.
A program may use at most 64 MiB of HBM per device.

```python
import math
import jax
import jax.numpy as jnp
from jax import lax

D_OUT = 4096
D_IN = 4096
RANK = 512
TOKENS = 1024
ROWS_MP = 1024
N_MP = 4


def block_scale(key, extent, shards, least, top_value):
    def one(axis_at, parts):
        heights = jax.random.uniform(jax.random.fold_in(jax.random.fold_in(key, 6), axis_at), (parts,), jnp.float32, least / len(shards), top_value / len(shards))
        return jnp.repeat(jnp.exp(heights), extent[axis_at] // parts).reshape((-1,) + (1,) * (len(extent) - axis_at - 1))

    loudness = one(*shards[0])
    for cut in shards[1:]:
        loudness = loudness * one(*cut)
    return loudness


def scatter_about(key, dims, deviation, bound, pieces=(), held_as=jnp.bfloat16):
    result = jax.random.normal(key, dims, jnp.float32) * deviation
    if len(pieces) > 0:
        result = block_scale(key, dims, pieces, -0.22, 0.18) * result
    return jnp.clip(result, min=-bound, max=bound).astype(held_as)


def setup_inputs(seed: int = 0) -> dict:
    arg_keys = jax.random.split(jax.random.key(seed), 7)
    return {
        "tokens": scatter_about(arg_keys[0], (2, TOKENS, D_IN), 1.0, 6.0, ((1, 8), (2, 4))),
        "targets": scatter_about(arg_keys[1], (2, TOKENS, D_OUT), 1.0, 6.0, ((1, 8), (2, 4))),
        "weight": scatter_about(arg_keys[2], (D_OUT, D_IN), D_IN ** -0.5, 0.09375, ((0, 4),)),
        "basis": scatter_about(arg_keys[3], (D_IN, RANK), D_IN ** -0.5, 0.09375),
        "moment1": scatter_about(arg_keys[4], (N_MP, ROWS_MP, RANK), 0.01, 0.06, ((0, 4), (1, 8)), jnp.float32),
        "moment2": jnp.clip(jnp.exp(math.log(0.001) - 4.6051703 * jax.random.uniform(arg_keys[5], (N_MP, ROWS_MP, RANK), jnp.float32) ** block_scale(arg_keys[5], (N_MP, ROWS_MP, RANK), ((0, 4), (1, 8)), -0.2, 0.2)), 9.999999747378752e-06, 0.001),
    }


def reference(tokens, targets, weight, basis, moment1, moment2):
    first = moment1.reshape(D_OUT, RANK)
    second = moment2.reshape(D_OUT, RANK)
    current = weight
    for turn in range(2):
        inputs = tokens[turn]
        outputs = jnp.dot(inputs, current.T, preferred_element_type=jnp.float32).astype(jnp.bfloat16)
        errors = (outputs.astype(jnp.float32) - targets[turn].astype(jnp.float32)).astype(jnp.bfloat16)
        reduced = jnp.dot(inputs, basis, preferred_element_type=jnp.float32)
        projected = jnp.dot(errors.astype(jnp.float32).T, reduced, precision=lax.Precision.HIGHEST) / TOKENS
        first = 0.9 * first + 0.1 * projected
        second = 0.95 * second + 0.05 * projected * projected
        direction = (first / (jnp.sqrt(second) + 1e-08)).astype(jnp.bfloat16)
        lifted = jnp.dot(direction, basis.T, preferred_element_type=jnp.float32)
        current = (current.astype(jnp.float32) - 0.02 * lifted).astype(jnp.bfloat16)
    return (current, first.reshape(N_MP, ROWS_MP, RANK), second.reshape(N_MP, ROWS_MP, RANK))
```

```python
import functools

import jax
import jax.numpy as jnp
from jax import lax
from jax.experimental import pallas as pl
from jax.experimental.pallas import tpu as pltpu
from jax.sharding import PartitionSpec as P

F32 = jnp.float32
BF16 = jnp.bfloat16


def dot_nt(a, b):
    return lax.dot_general(a, b, (((1,), (1,)), ((), ())), preferred_element_type=F32)


def dot_tn(a, b):
    return lax.dot_general(a, b, (((0,), (0,)), ((), ())), preferred_element_type=F32)


def kernel(
    n_dp, n_mp, total_tokens,
    tok, tgt_hbm, w_hbm, b_hbm, m_hbm, v_hbm,
    w1_hbm, d1_hbm, m_out, v_out,
    xbuf, tgt, w, b, mom1, mom2, y, r, e, g, send1, recv1, send2, recv2, dall,
    l_sem, x_send, x_recv, s1_send, s1_recv, s2_send, s2_recv, d_send, d_recv, o_sem,
):
    dp = lax.axis_index("dp")
    mp = lax.axis_index("mp")
    core = lax.rem(dp, 2)
    chip = lax.div(dp, 2)
    partner = dp + 1 - 2 * core
    n_ch = n_dp // 2
    out_rows, features = w_hbm.shape
    rows = out_rows // n_dp
    fin = features // n_mp
    rank = b_hbm.shape[1]
    tile = min(256, out_rows)
    tiles = out_rows // tile

    def mp_at(k):
        return lax.rem(mp + k, n_mp)

    def chip_at(k):
        return lax.rem(chip + k, n_ch)

    def columns(j):
        return pl.ds(pl.multiple_of(j * fin, fin), fin)

    def owner_rows(i):
        return pl.ds(pl.multiple_of(i * rows, rows), rows)

    def tile_at(i):
        return pl.ds(pl.multiple_of(i * tile, tile), tile)

    def remote(src, dst, send, recv, where):
        return pltpu.make_async_remote_copy(
            src_ref=src, dst_ref=dst, send_sem=send, recv_sem=recv,
            device_id=where, device_id_type=pl.DeviceIdType.MESH,
        )

    w_copies = []
    for k in range(n_mp):
        j = mp_at(k)
        w_copies.append(pltpu.make_async_copy(w_hbm.at[:, columns(j)], w.at[j], l_sem.at[k]))
    b_copy = pltpu.make_async_copy(b_hbm, b, l_sem.at[n_mp])
    t_copy = pltpu.make_async_copy(tgt_hbm, tgt, l_sem.at[n_mp + 1])
    m_copy = pltpu.make_async_copy(m_hbm.at[0], mom1, l_sem.at[n_mp + 2])
    v_copy = pltpu.make_async_copy(v_hbm.at[0], mom2, l_sem.at[n_mp + 3])
    b_copy.start()
    for copy in w_copies:
        copy.start()
    t_copy.start()
    m_copy.start()
    v_copy.start()

    barrier = pltpu.get_barrier_semaphore()
    peers = [(dp, mp_at(k)) for k in range(1, n_mp)]
    peers += [(chip_at(k) * 2 + core, mp) for k in range(1, n_ch)]
    peers += [(partner, mp)]
    for peer in peers:
        pl.semaphore_signal(barrier, inc=1, device_id=peer, device_id_type=pl.DeviceIdType.MESH)
    pl.semaphore_wait(barrier, len(peers))

    sends = []
    for s in range(2):
        for k in range(1, n_mp):
            copy = remote(
                tok.at[s], xbuf.at[s, mp], x_send.at[s, k], x_recv.at[s, mp], (dp, mp_at(k))
            )
            copy.start()
            sends.append(copy)

    def block(s, j, x, first):
        @pl.loop(0, tiles)
        def _(i):
            term = dot_nt(x[...], w[j, tile_at(i), :])
            if first:
                y[s, :, tile_at(i)] = term
            else:
                y[s, :, tile_at(i)] += term

        term = jnp.dot(x[...], b[columns(j), :], preferred_element_type=F32)
        if first:
            r[s] = term
        else:
            r[s] += term

    def arrive(s, k):
        j = mp_at(k)
        remote(
            tok.at[s], xbuf.at[s, j], x_send.at[s, k], x_recv.at[s, j], (dp, j)
        ).wait_recv()
        block(s, j, xbuf.at[s, j], False)

    def gradient(s):
        reduced = r[s].astype(BF16)

        @pl.loop(0, tiles)
        def _(i):
            outputs = y[s, :, tile_at(i)]
            if s == 1:
                outputs = outputs - 0.02 * dot_nt(reduced, dall[0, tile_at(i), :])
            outputs = outputs.astype(BF16).astype(F32)
            e[:, tile_at(i)] = (outputs - tgt[s, :, tile_at(i)].astype(F32)).astype(BF16)
            g[tile_at(i), :] = dot_tn(e[:, tile_at(i)], reduced)

    def scatter_start(s):
        ones = []
        for k in range(1, n_ch + 1):
            c = chip_at(k)
            send1[s, c] = g[owner_rows(c * 2 + 1 - core), :].astype(BF16)
            copy = remote(
                send1.at[s, c], recv1.at[s, c], s1_send.at[s, c], s1_recv.at[s, c], (partner, mp)
            )
            copy.start()
            sends.append(copy)
            ones.append((c, copy))
        for k, (c, copy) in enumerate(ones):
            copy.wait_recv()
            total = g[owner_rows(c * 2 + core), :] + recv1[s, c].astype(F32)
            if k < n_ch - 1:
                send2[s, c] = total.astype(BF16)
                out = remote(
                    send2.at[s, c], recv2.at[s, chip], s2_send.at[s, c], s2_recv.at[s, chip],
                    (c * 2 + core, mp),
                )
                out.start()
                sends.append(out)
            else:
                g[owner_rows(c * 2 + core), :] = total

    def scatter_finish(s):
        total = g[owner_rows(dp), :]
        for k in range(1, n_ch):
            c = chip_at(k)
            remote(
                send2.at[s, c], recv2.at[s, c], s2_send.at[s, c], s2_recv.at[s, c],
                (c * 2 + core, mp),
            ).wait_recv()
            total = total + recv2[s, c].astype(F32)
        projected = total / total_tokens
        first = 0.9 * mom1[...] + 0.1 * projected
        second = 0.95 * mom2[...] + 0.05 * projected * projected
        mom1[...] = first
        mom2[...] = second
        dall[s, owner_rows(dp), :] = (first / (jnp.sqrt(second) + 1e-08)).astype(BF16)

    def direction_copy(s, owner, sem_at, where):
        part = dall.at[s, owner_rows(owner), :]
        return remote(part, part, d_send.at[s, sem_at], d_recv.at[s, owner], where)

    def gather_start(s):
        for k in range(1, n_ch):
            c = chip_at(k)
            copy = direction_copy(s, dp, c, (c * 2 + core, mp))
            copy.start()
            sends.append(copy)
        copy = direction_copy(s, dp, n_ch + chip, (partner, mp))
        copy.start()
        sends.append(copy)

    def gather_forward(s):
        for k in range(1, n_ch):
            c = chip_at(k)
            owner = c * 2 + core
            direction_copy(s, owner, c, (owner, mp)).wait_recv()
            copy = direction_copy(s, owner, n_ch + c, (partner, mp))
            copy.start()
            sends.append(copy)

    def gather_finish(s):
        for k in range(n_ch):
            c = chip_at(k)
            direction_copy(s, c * 2 + 1 - core, n_ch + c, (partner, mp)).wait_recv()

    def lift(j):
        @pl.loop(0, tiles)
        def _(i):
            lifted = dot_nt(dall[0, tile_at(i), :], b[j * fin:(j + 1) * fin, :])
            w[j, tile_at(i), :] = (w[j, tile_at(i), :].astype(F32) - 0.02 * lifted).astype(BF16)

        copy = pltpu.make_async_copy(
            w.at[j], w1_hbm.at[:, j * fin:(j + 1) * fin], o_sem.at[j]
        )
        copy.start()
        return copy

    b_copy.wait()
    w_copies[0].wait()
    block(0, mp, tok.at[0], True)
    block(1, mp, tok.at[1], True)
    for copy in w_copies[1:]:
        copy.wait()
    t_copy.wait()
    m_copy.wait()
    v_copy.wait()
    for k in range(1, n_mp):
        arrive(0, k)
    gradient(0)
    scatter_start(0)
    scatter_finish(0)
    gather_start(0)
    gather_forward(0)
    for k in range(1, n_mp):
        arrive(1, k)
    gather_finish(0)
    gradient(1)
    scatter_start(1)
    outs = [lift(j) for j in range(n_mp)]
    scatter_finish(1)
    gather_start(1)
    m_done = pltpu.make_async_copy(mom1, m_out.at[0], o_sem.at[n_mp])
    v_done = pltpu.make_async_copy(mom2, v_out.at[0], o_sem.at[n_mp + 1])
    m_done.start()
    v_done.start()
    gather_forward(1)
    gather_finish(1)
    d_done = pltpu.make_async_copy(dall.at[1], d1_hbm, o_sem.at[n_mp + 2])
    d_done.start()
    for copy in sends:
        copy.wait_send()
    for copy in outs:
        copy.wait()
    m_done.wait()
    v_done.wait()
    d_done.wait()


def local(n_dp, n_mp, tokens, targets, weight, basis, moment1, moment2):
    steps, toks, fin = tokens.shape
    out_rows, features = weight.shape
    rank = basis.shape[1]
    rows = moment1.shape[1]
    n_ch = n_dp // 2
    hbm = pl.BlockSpec(memory_space=pl.ANY)
    dma = pltpu.SemaphoreType.DMA
    w1, d1, first, second = pl.pallas_call(
        functools.partial(kernel, n_dp, n_mp, toks * n_dp),
        out_shape=(
            jax.ShapeDtypeStruct((out_rows, features), BF16),
            jax.ShapeDtypeStruct((out_rows, rank), BF16),
            jax.ShapeDtypeStruct((1, rows, rank), F32),
            jax.ShapeDtypeStruct((1, rows, rank), F32),
        ),
        in_specs=[pl.BlockSpec(memory_space=pltpu.VMEM)] + [hbm] * 5,
        out_specs=(hbm,) * 4,
        scratch_shapes=[
            pltpu.VMEM((steps, n_mp, toks, fin), BF16),
            pltpu.VMEM((steps, toks, out_rows), BF16),
            pltpu.VMEM((n_mp, out_rows, fin), BF16),
            pltpu.VMEM((features, rank), BF16),
            pltpu.VMEM((rows, rank), F32),
            pltpu.VMEM((rows, rank), F32),
            pltpu.VMEM((steps, toks, out_rows), F32),
            pltpu.VMEM((steps, toks, rank), F32),
            pltpu.VMEM((toks, out_rows), BF16),
            pltpu.VMEM((out_rows, rank), F32),
            pltpu.VMEM((steps, n_ch, rows, rank), BF16),
            pltpu.VMEM((steps, n_ch, rows, rank), BF16),
            pltpu.VMEM((steps, n_ch, rows, rank), BF16),
            pltpu.VMEM((steps, n_ch, rows, rank), BF16),
            pltpu.VMEM((steps, out_rows, rank), BF16),
            dma((n_mp + 4,)),
            dma((steps, n_mp)),
            dma((steps, n_mp)),
            dma((steps, n_ch)),
            dma((steps, n_ch)),
            dma((steps, n_ch)),
            dma((steps, n_ch)),
            dma((steps, n_dp)),
            dma((steps, n_dp)),
            dma((n_mp + 3,)),
        ],
        compiler_params=pltpu.CompilerParams(
            collective_id=0, has_side_effects=True, vmem_limit_bytes=48 * 2**20
        ),
    )(tokens, targets, weight, basis, moment1, moment2)
    lifted = lax.dot_general(
        d1, basis, (((1,), (1,)), ((), ())), preferred_element_type=F32
    )
    return ((w1.astype(F32) - 0.02 * lifted).astype(BF16), first, second)


def solution(mesh):
    in_specs = (
        P(None, "dp", "mp"),
        P(None, "dp", "mp"),
        P("mp", None),
        P(),
        P("mp", "dp", None),
        P("mp", "dp", None),
    )
    out_specs = (P("mp", None), P("mp", "dp", None), P("mp", "dp", None))
    body = functools.partial(local, mesh.shape["dp"], mesh.shape["mp"])
    return jax.shard_map(body, mesh=mesh, in_specs=in_specs, out_specs=out_specs, check_vma=False)
```

```python
import functools

import jax
import jax.numpy as jnp
from jax import lax
from jax.experimental import pallas as pl
from jax.experimental.pallas import tpu as pltpu
from jax.sharding import PartitionSpec as P

F32 = jnp.float32
BF16 = jnp.bfloat16


def dot_nt(a, b):
    return lax.dot_general(a, b, (((1,), (1,)), ((), ())), preferred_element_type=F32)


def dot_tn(a, b):
    return lax.dot_general(a, b, (((0,), (0,)), ((), ())), preferred_element_type=F32)


def kernel(
    n_dp, n_mp, total_tokens,
    tok, tgt_hbm, w_hbm, b_hbm, m_hbm, v_hbm,
    w1_hbm, d1_hbm, m_out, v_out,
    xbuf, tgt, w, b, mom1, mom2, y, r, e, g, send1, recv1, send2, recv2, dall,
    l_sem, x_send, x_recv, s1_send, s1_recv, s2_send, s2_recv, d_send, d_recv, o_sem,
):
    dp = lax.axis_index("dp")
    mp = lax.axis_index("mp")
    core = lax.rem(dp, 2)
    chip = lax.div(dp, 2)
    partner = dp + 1 - 2 * core
    n_ch = n_dp // 2
    out_rows, features = w_hbm.shape
    rows = out_rows // n_dp
    fin = features // n_mp
    rank = b_hbm.shape[1]
    tile = min(256, out_rows)
    tiles = out_rows // tile

    def mp_at(k):
        return lax.rem(mp + k, n_mp)

    def chip_at(k):
        return lax.rem(chip + k, n_ch)

    def columns(j):
        return pl.ds(pl.multiple_of(j * fin, fin), fin)

    def owner_rows(i):
        return pl.ds(pl.multiple_of(i * rows, rows), rows)

    def tile_at(i):
        return pl.ds(pl.multiple_of(i * tile, tile), tile)

    def remote(src, dst, send, recv, where):
        return pltpu.make_async_remote_copy(
            src_ref=src, dst_ref=dst, send_sem=send, recv_sem=recv,
            device_id=where, device_id_type=pl.DeviceIdType.MESH,
        )

    w_copies = []
    for k in range(n_mp):
        j = mp_at(k)
        w_copies.append(pltpu.make_async_copy(w_hbm.at[:, columns(j)], w.at[j], l_sem.at[k]))
    b_copy = pltpu.make_async_copy(b_hbm, b, l_sem.at[n_mp])
    t_copy = pltpu.make_async_copy(tgt_hbm, tgt, l_sem.at[n_mp + 1])
    m_copy = pltpu.make_async_copy(m_hbm.at[0], mom1, l_sem.at[n_mp + 2])
    v_copy = pltpu.make_async_copy(v_hbm.at[0], mom2, l_sem.at[n_mp + 3])
    k_copy = pltpu.make_async_copy(tok, xbuf.at[:, mp], l_sem.at[n_mp + 4])
    k_copy.start()
    b_copy.start()
    for copy in w_copies:
        copy.start()
    t_copy.start()
    m_copy.start()
    v_copy.start()

    barrier = pltpu.get_barrier_semaphore()
    peers = [(dp, mp_at(k)) for k in range(1, n_mp)]
    peers += [(chip_at(k) * 2 + core, mp) for k in range(1, n_ch)]
    peers += [(partner, mp)]
    for peer in peers:
        pl.semaphore_signal(barrier, inc=1, device_id=peer, device_id_type=pl.DeviceIdType.MESH)
    pl.semaphore_wait(barrier, len(peers))

    def token_copy(s, j, lane, where):
        part = xbuf.at[s, j]
        return remote(part, part, x_send.at[s, lane], x_recv.at[s, j], (dp, where))

    def relay(d, down):
        j = mp + d if down else mp - d
        there = (j < n_mp) if down else (j >= 0)
        onward = (mp > 0) if down else (mp < n_mp - 1)
        to = mp - 1 if down else mp + 1
        return j, there, onward, token_copy(0, j, 2 * d + int(down), to)

    def relay_step(d, down):
        j, there, onward, copy = relay(d, down)

        @pl.when(there)
        def _():
            if d > 0:
                copy.wait_recv()

            @pl.when(onward)
            def _():
                copy.start()

    def relay_done(d, down):
        j, there, onward, copy = relay(d, down)

        @pl.when(jnp.logical_and(there, onward))
        def _():
            copy.wait_send()

    low = (mp < n_mp // 2).astype(jnp.int32)

    def other_at(i):
        down = n_mp - 1 - i
        down = down - (down <= mp).astype(jnp.int32)
        up = i + (mp <= i).astype(jnp.int32)
        return low * down + (1 - low) * up

    sends = []
    k_copy.wait()
    for d in range(n_mp):
        for down in (True, False):
            relay_step(d, down)
    for i in range(n_mp - 1):
        copy = token_copy(1, mp, i, other_at(i))
        copy.start()
        sends.append(copy)

    def block(s, j, x, first):
        @pl.loop(0, tiles)
        def _(i):
            term = dot_nt(x[...], w[j, tile_at(i), :])
            if first:
                y[s, :, tile_at(i)] = term
            else:
                y[s, :, tile_at(i)] += term

        term = jnp.dot(x[...], b[columns(j), :], preferred_element_type=F32)
        if first:
            r[s] = term
        else:
            r[s] += term

    def arrive(s, i):
        j = other_at(i)
        if s == 1:
            token_copy(1, j, i, j).wait_recv()
        block(s, j, xbuf.at[s, j], False)

    def gradient(s):
        reduced = r[s].astype(BF16)

        @pl.loop(0, tiles)
        def _(i):
            outputs = y[s, :, tile_at(i)]
            if s == 1:
                outputs = outputs - 0.02 * dot_nt(reduced, dall[0, tile_at(i), :])
            outputs = outputs.astype(BF16).astype(F32)
            e[:, tile_at(i)] = (outputs - tgt[s, :, tile_at(i)].astype(F32)).astype(BF16)
            g[tile_at(i), :] = dot_tn(e[:, tile_at(i)], reduced)

    def scatter_start(s):
        ones = []
        for k in range(1, n_ch + 1):
            c = chip_at(k)
            send1[s, c] = g[owner_rows(c * 2 + 1 - core), :].astype(BF16)
            copy = remote(
                send1.at[s, c], recv1.at[s, c], s1_send.at[s, c], s1_recv.at[s, c], (partner, mp)
            )
            copy.start()
            sends.append(copy)
            ones.append((c, copy))
        for k, (c, copy) in enumerate(ones):
            copy.wait_recv()
            total = g[owner_rows(c * 2 + core), :] + recv1[s, c].astype(F32)
            if k < n_ch - 1:
                send2[s, c] = total.astype(BF16)
                out = remote(
                    send2.at[s, c], recv2.at[s, chip], s2_send.at[s, c], s2_recv.at[s, chip],
                    (c * 2 + core, mp),
                )
                out.start()
                sends.append(out)
            else:
                g[owner_rows(c * 2 + core), :] = total

    def scatter_finish(s):
        total = g[owner_rows(dp), :]
        for k in range(1, n_ch):
            c = chip_at(k)
            remote(
                send2.at[s, c], recv2.at[s, c], s2_send.at[s, c], s2_recv.at[s, c],
                (c * 2 + core, mp),
            ).wait_recv()
            total = total + recv2[s, c].astype(F32)
        projected = total / total_tokens
        first = 0.9 * mom1[...] + 0.1 * projected
        second = 0.95 * mom2[...] + 0.05 * projected * projected
        mom1[...] = first
        mom2[...] = second
        dall[s, owner_rows(dp), :] = (first / (jnp.sqrt(second) + 1e-08)).astype(BF16)

    def direction_copy(s, owner, sem_at, where):
        part = dall.at[s, owner_rows(owner), :]
        return remote(part, part, d_send.at[s, sem_at], d_recv.at[s, owner], where)

    def gather_start(s):
        for k in range(1, n_ch):
            c = chip_at(k)
            copy = direction_copy(s, dp, c, (c * 2 + core, mp))
            copy.start()
            sends.append(copy)
        copy = direction_copy(s, dp, n_ch + chip, (partner, mp))
        copy.start()
        sends.append(copy)

    def gather_forward(s):
        for k in range(1, n_ch):
            c = chip_at(k)
            owner = c * 2 + core
            direction_copy(s, owner, c, (owner, mp)).wait_recv()
            copy = direction_copy(s, owner, n_ch + c, (partner, mp))
            copy.start()
            sends.append(copy)

    def gather_finish(s):
        for k in range(n_ch):
            c = chip_at(k)
            direction_copy(s, c * 2 + 1 - core, n_ch + c, (partner, mp)).wait_recv()

    def lift(j):
        width = min(256, fin)

        @pl.loop(0, fin // width)
        def _(i):
            cols = pl.ds(pl.multiple_of(i * width, width), width)
            from_b = pl.ds(pl.multiple_of(j * fin + i * width, width), width)
            lifted = dot_nt(dall[0], b[from_b, :])
            w[j, :, cols] = (w[j, :, cols].astype(F32) - 0.02 * lifted).astype(BF16)

        copy = pltpu.make_async_copy(
            w.at[j], w1_hbm.at[:, j * fin:(j + 1) * fin], o_sem.at[j]
        )
        copy.start()
        return copy

    b_copy.wait()
    for copy in w_copies:
        copy.wait()
    block(0, mp, xbuf.at[0, mp], True)
    t_copy.wait()
    m_copy.wait()
    v_copy.wait()
    for i in reversed(range(n_mp - 1)):
        arrive(0, i)
    gradient(0)
    scatter_start(0)
    scatter_finish(0)
    gather_start(0)
    block(1, mp, xbuf.at[1, mp], True)
    gather_forward(0)
    for i in reversed(range(n_mp - 1)):
        arrive(1, i)
    gather_finish(0)
    gradient(1)
    scatter_start(1)
    outs = [lift(j) for j in range(n_mp)]
    scatter_finish(1)
    gather_start(1)
    m_done = pltpu.make_async_copy(mom1, m_out.at[0], o_sem.at[n_mp])
    v_done = pltpu.make_async_copy(mom2, v_out.at[0], o_sem.at[n_mp + 1])
    m_done.start()
    v_done.start()
    gather_forward(1)
    gather_finish(1)
    d_done = pltpu.make_async_copy(dall.at[1], d1_hbm, o_sem.at[n_mp + 2])
    d_done.start()
    for copy in sends:
        copy.wait_send()
    for d in range(n_mp):
        for down in (True, False):
            relay_done(d, down)
    for copy in outs:
        copy.wait()
    m_done.wait()
    v_done.wait()
    d_done.wait()


def last_lift(width, w1, d1, b, first, second, w_out, m_out, v_out, stage, sem, s_sem):
    m_copy = pltpu.make_async_copy(first, m_out, s_sem.at[0])
    v_copy = pltpu.make_async_copy(second, v_out, s_sem.at[1])
    m_copy.start()
    v_copy.start()
    features = w1.shape[1]
    count = features // width

    def put(i, slot):
        at = pl.ds(pl.multiple_of(i * width, width), width)
        return pltpu.make_async_copy(stage.at[slot], w_out.at[:, at], sem.at[slot])

    @pl.loop(0, count)
    def _(i):
        slot = lax.rem(i, 2)

        @pl.when(i >= 2)
        def _():
            put(i - 2, slot).wait()

        at = pl.ds(pl.multiple_of(i * width, width), width)
        lifted = dot_nt(d1[...], b[at, :])
        stage[slot] = (w1[:, at].astype(F32) - 0.02 * lifted).astype(BF16)
        put(i, slot).start()

    for i in range(max(count - 2, 0), count):
        put(i, i % 2).wait()
    m_copy.wait()
    v_copy.wait()


def local(n_dp, n_mp, tokens, targets, weight, basis, moment1, moment2):
    steps, toks, fin = tokens.shape
    out_rows, features = weight.shape
    rank = basis.shape[1]
    rows = moment1.shape[1]
    n_ch = n_dp // 2
    hbm = pl.BlockSpec(memory_space=pltpu.HBM)
    anywhere = pl.BlockSpec(memory_space=pl.ANY)
    dma = pltpu.SemaphoreType.DMA
    w1, d1, first, second = pl.pallas_call(
        functools.partial(kernel, n_dp, n_mp, toks * n_dp),
        out_shape=(
            jax.ShapeDtypeStruct((out_rows, features), BF16),
            jax.ShapeDtypeStruct((out_rows, rank), BF16),
            jax.ShapeDtypeStruct((1, rows, rank), F32),
            jax.ShapeDtypeStruct((1, rows, rank), F32),
        ),
        in_specs=[hbm] * 6,
        out_specs=(anywhere,) * 4,
        scratch_shapes=[
            pltpu.VMEM((steps, n_mp, toks, fin), BF16),
            pltpu.VMEM((steps, toks, out_rows), BF16),
            pltpu.VMEM((n_mp, out_rows, fin), BF16),
            pltpu.VMEM((features, rank), BF16),
            pltpu.VMEM((rows, rank), F32),
            pltpu.VMEM((rows, rank), F32),
            pltpu.VMEM((steps, toks, out_rows), F32),
            pltpu.VMEM((steps, toks, rank), F32),
            pltpu.VMEM((toks, out_rows), BF16),
            pltpu.VMEM((out_rows, rank), F32),
            pltpu.VMEM((steps, n_ch, rows, rank), BF16),
            pltpu.VMEM((steps, n_ch, rows, rank), BF16),
            pltpu.VMEM((steps, n_ch, rows, rank), BF16),
            pltpu.VMEM((steps, n_ch, rows, rank), BF16),
            pltpu.VMEM((steps, out_rows, rank), BF16),
            dma((n_mp + 5,)),
            dma((steps, 2 * n_mp)),
            dma((steps, n_mp)),
            dma((steps, n_ch)),
            dma((steps, n_ch)),
            dma((steps, n_ch)),
            dma((steps, n_ch)),
            dma((steps, n_dp)),
            dma((steps, n_dp)),
            dma((n_mp + 3,)),
        ],
        compiler_params=pltpu.CompilerParams(
            collective_id=0, has_side_effects=True, vmem_limit_bytes=36 * 2**20
        ),
    )(*[
        pltpu.with_memory_space_constraint(x, pltpu.HBM)
        for x in (tokens, targets, weight, basis, moment1, moment2)
    ])
    width = min(256, features)
    vmem = pl.BlockSpec(memory_space=pltpu.VMEM)
    return pl.pallas_call(
        functools.partial(last_lift, width),
        out_shape=(
            jax.ShapeDtypeStruct((out_rows, features), BF16),
            jax.ShapeDtypeStruct((1, rows, rank), F32),
            jax.ShapeDtypeStruct((1, rows, rank), F32),
        ),
        in_specs=[vmem] * 5,
        out_specs=(hbm,) * 3,
        scratch_shapes=[pltpu.VMEM((2, out_rows, width), BF16), dma((2,)), dma((2,))],
        compiler_params=pltpu.CompilerParams(vmem_limit_bytes=12 * 2**20),
    )(w1, d1, basis, first, second)


def solution(mesh):
    in_specs = (
        P(None, "dp", "mp"),
        P(None, "dp", "mp"),
        P("mp", None),
        P(),
        P("mp", "dp", None),
        P("mp", "dp", None),
    )
    out_specs = (P("mp", None), P("mp", "dp", None), P("mp", "dp", None))
    body = functools.partial(local, mesh.shape["dp"], mesh.shape["mp"])
    return jax.shard_map(body, mesh=mesh, in_specs=in_specs, out_specs=out_specs, check_vma=False)
```
